1024 devices in a mesh: fsdp: 64 (over x_lo, z), tp: 16 (over x_hi, y, core).
Axes of the slice: x: 4 (x_hi: 2, x_lo: 2; x = x_hi * 2 + x_lo), y: 4, z: 32, core: 2. Of those that a mesh axis runs over, the one named last changes fastest.
Arguments:
- dec_query: bfloat16 [64, 2, 4096], P('fsdp'), may hold values from -200 to 200
- new_keys: bfloat16 [64, 2, 512], P('fsdp'), may hold values from -6 to 6
- new_values: bfloat16 [64, 2, 512], P('fsdp'), may hold values from -6 to 6
- cache_keys: bfloat16 [64, 2048, 512], P('fsdp', 'tp'), may hold values from -6 to 6
- cache_values: bfloat16 [64, 2048, 512], P('fsdp', 'tp'), may hold values from -6 to 6
- lengths: int32 [64], P('fsdp'), may hold values from 256 to 2048, as said below
- out_weight: bfloat16 [4096, 4096], P('fsdp', 'tp'), may hold values from -0.09375 to 0.09375
- train_attn: bfloat16 [8192, 4096], P('fsdp', 'tp'), may hold values from -0.15625 to 0.15625
- grad_out: bfloat16 [8192, 4096], P('fsdp'), may hold values from -16 to 16
Outputs:
- dec_out: bfloat16 [64, 2, 4096], P('fsdp', None, 'tp')
- grad_attn: bfloat16 [8192, 4096], P('fsdp', 'tp')
- grad_weight: float32 [4096, 4096], P('fsdp', 'tp')
The draws below stay inside these ranges and needn't reach their ends.
Inputs may be any that keep to these rules, and one draw needn't show every extreme that they name: `lengths`: the length 2048 occurs.
All inputs are finite; a program needn't handle non-finite values.
Results may differ from the reference program's by a relative error of at most 0.0049.
Values may be sent and summed in bfloat16 or wider, within the bound.
A program may use at most 32 MiB of HBM per device.

```python
import jax
import jax.numpy as jnp
from jax import lax

DOUT = 4096
QH = 32
KVH = 4
HD = 128
CACHE = 2048
STEPS = 2
GROUP = 8
QW = 4096
KVW = 512
DEC_ROWS = 64
TOKENS = 8192


def decode_pair(key):
    key_draw = jax.random.truncated_normal(jax.random.fold_in(key, 101), -6.0, 6.0, (DEC_ROWS, STEPS, KVH, HD), jnp.float32)
    jitter = jax.random.truncated_normal(jax.random.fold_in(key, 102), -6.0, 6.0, (DEC_ROWS, STEPS, KVH, GROUP, HD), jnp.float32)
    queries = 2.5 * jitter + 0.7 * key_draw[:, :, :, None, :]
    return (key_draw.reshape(DEC_ROWS, STEPS, KVH * HD), queries.reshape(DEC_ROWS, STEPS, QH * HD))


def draw_dec_query(key, part):
    return decode_pair(key)[1].astype(jnp.bfloat16)


def draw_new_keys(key, part):
    return decode_pair(key)[0].astype(jnp.bfloat16)


def draw_lengths(key, part):
    lengths_drawn = jax.random.randint(jax.random.fold_in(key, 201), (DEC_ROWS,), CACHE // 8, CACHE + 1, dtype=jnp.int32)
    shuffled = jax.random.permutation(jax.random.fold_in(key, 202), DEC_ROWS)
    lengths_drawn = lengths_drawn.at[shuffled[0]].set(CACHE)
    lengths_drawn = lengths_drawn.at[shuffled[1]].set(CACHE // 8)
    return lengths_drawn


def spiked(result, stream_key, source, target, shards_of, factor):
    def block_of(position):
        return (jnp.arange(result.shape[position]) // (result.shape[position] // shards_of)).reshape((-1,) + (1,) * (result.ndim - 1 - position))

    one_side = jax.random.permutation(stream_key, shards_of)[block_of(target)]
    far = (block_of(target) + shards_of // 2) % shards_of
    return jnp.where((block_of(source) == one_side) | (block_of(source) == far), factor * result, result)


def steps_of(stream_key, shape, pieces, smallest, top_value):
    def one(position, blocks):
        heights = jax.random.uniform(jax.random.fold_in(jax.random.fold_in(stream_key, 6), position), (blocks,), jnp.float32, smallest / len(pieces), top_value / len(pieces))
        return jnp.repeat(jnp.exp(heights), shape[position] // blocks).reshape((-1,) + (1,) * (len(shape) - position - 1))

    loudness = one(*pieces[0])
    for cut in pieces[1:]:
        loudness = loudness * one(*cut)
    return loudness


def noise(key, shape, deviation, reach, shards=(), kind=jnp.bfloat16):
    result = jax.random.normal(key, shape, jnp.float32) * deviation
    if len(shards) > 0:
        result = steps_of(key, shape, shards, -0.22, 0.18) * result
    return jnp.clip(result, min=-reach, max=reach).astype(kind)


def gaussian_with(key, extent, scale, most, cuts, heavy, kind=jnp.bfloat16):
    values = scale * jax.random.normal(key, extent, jnp.float32)
    if cuts:
        values = values * steps_of(key, extent, cuts, -0.22, 0.18)
    return jnp.clip(spiked(values, jax.random.fold_in(key, 3), *heavy), -most, most).astype(kind)


def setup_inputs(seed: int = 0) -> dict:
    keys = jax.random.split(jax.random.key(seed), 10)
    dec_query = draw_dec_query(jax.random.fold_in(keys[9], 71), 0)
    new_keys = draw_new_keys(jax.random.fold_in(keys[9], 71), 0)
    new_values = noise(keys[2], (DEC_ROWS, STEPS, KVW), 1.0, 6.0, ((0, 64),))
    cache_keys = noise(keys[3], (DEC_ROWS, CACHE, KVW), 1.0, 6.0, ((0, 64), (1, 16)))
    cache_values = noise(keys[4], (DEC_ROWS, CACHE, KVW), 1.0, 6.0, ((0, 64), (1, 16)))
    lengths = draw_lengths(jax.random.fold_in(keys[9], 71), 0)
    out_weight = noise(keys[6], (DOUT, QW), QW ** -0.5, 0.09375, ((0, 64), (1, 16)))
    train_attn = noise(keys[7], (TOKENS, QW), (TOKENS ** -0.5), 0.15625, ((0, 64), (1, 16)))
    grad_out = gaussian_with(keys[8], (TOKENS, DOUT), 1.0, 16.0, ((0, 64),), (0, 1, 64, 4.0))
    return {"dec_query": dec_query, "new_keys": new_keys, "new_values": new_values, "cache_keys": cache_keys, "cache_values": cache_values, "lengths": lengths, "out_weight": out_weight, "train_attn": train_attn, "grad_out": grad_out}


def reference(dec_query, new_keys, new_values, cache_keys, cache_values, lengths, out_weight, train_attn, grad_out):
    scaling = 1.0 / (HD ** 0.5)
    step_allowed = jnp.arange(STEPS, dtype=jnp.int32)[None, :] <= jnp.arange(STEPS, dtype=jnp.int32)[:, None]

    def one_row(record):
        queries, key_new, value_new, key_cache, value_cache, length = record
        q_float = queries.astype(jnp.float32).reshape(STEPS, KVH, GROUP, HD)
        all_keys = jnp.concatenate([key_cache, key_new], axis=0).astype(jnp.float32).reshape(CACHE + STEPS, KVH, HD)
        all_values = jnp.concatenate([value_cache, value_new], axis=0).astype(jnp.float32).reshape(CACHE + STEPS, KVH, HD)
        cache_allowed = jnp.arange(CACHE, dtype=jnp.int32) < length
        allowed = jnp.concatenate([jnp.broadcast_to(cache_allowed[None, :], (STEPS, CACHE)), step_allowed], axis=1)
        scores = jnp.einsum("sgqd,pgd->sgqp", q_float, all_keys, precision=lax.Precision.HIGHEST) * scaling
        usable = allowed[:, None, None, :]
        maxima = jnp.max(jnp.where(usable, scores, -jnp.inf), axis=-1, keepdims=True)
        exp_terms = jnp.where(usable, jnp.exp(scores - maxima), jnp.float32(0.0))
        weighted = jnp.einsum("sgqp,pgd->sgqd", exp_terms, all_values, precision=lax.Precision.HIGHEST)
        attended = weighted / jnp.sum(exp_terms, axis=-1)[..., None]
        return attended.reshape(STEPS, QW).astype(jnp.bfloat16)

    dec_attn = lax.map(one_row, (dec_query, new_keys, new_values, cache_keys, cache_values, lengths))
    dec_out = jnp.dot(dec_attn.reshape(DEC_ROWS * STEPS, QW), out_weight.T, preferred_element_type=jnp.float32)
    dec_out = dec_out.reshape(DEC_ROWS, STEPS, DOUT).astype(jnp.bfloat16)
    grad_attn = jnp.dot(grad_out, out_weight, preferred_element_type=jnp.float32).astype(jnp.bfloat16)
    grad_weight = jnp.dot(grad_out.T, train_attn, preferred_element_type=jnp.float32)
    return dec_out, grad_attn, grad_weight
```

```python
import functools

import jax
import jax.numpy as jnp
from jax import lax
from jax.experimental import pallas as pl
from jax.experimental.pallas import tpu as pltpu
from jax.sharding import PartitionSpec as P

HD = 128
NEG_FILL = -1e30
MESH = pl.DeviceIdType.MESH
F32 = jnp.float32
BF16 = jnp.bfloat16
NEAR = BF16
NARROW_HOPS = 4


def kernel(
    fs, tp,
    q_hbm, nk_hbm, nv_hbm, ck_hbm, cv_hbm, len_ref, w_hbm, ta_hbm, g_hbm,
    dec_ref, ga_ref, gw_ref,
    q_ref, nk_ref, nv_ref, ck_ref, cv_ref, ta2, g_ref, in_s,
    wfull, part, gacc, gin, nbs, nbr, snd16, rcv16, snd32, rcv32, qs, att, sa, ra, sb, rb,
    ag_s, ag_r, fw_s, fw_r, ax_s, ax_r, nb_s, nb_r, rs_s, rs_r, g_s, g_r, t_s, t_r, a_s, a_r, b_s, b_r,
):
    ring = fs // 2
    half = ring // 2
    hops = half // 2
    rows = w_hbm.shape[0]
    cols = w_hbm.shape[1]
    tokens = ta_hbm.shape[0]
    hcols = cols // 2
    steps = q_ref.shape[1]
    heads = q_ref.shape[2] // HD
    kv_heads = nk_ref.shape[2] // HD
    group = heads // kv_heads
    heads_dev = heads // tp
    unit = heads_dev * steps
    dout = fs * rows
    dcols = dout // tp
    span = ring * rows

    f = lax.axis_index("fsdp")
    t = lax.axis_index("tp")
    xl = f // ring
    z = f % ring
    zp = (xl * ring + (z + 1) % ring, t)
    zm = (xl * ring + (z + ring - 1) % ring, t)
    zp2 = (xl * ring + (z + 2) % ring, t)
    zm2 = (xl * ring + (z + ring - 2) % ring, t)
    xp = ((f + ring) % fs, t)
    gp = ((f + ring) % fs, (t + tp // 2) % tp)

    def peer(k):
        return (t + k) % tp

    own_rows = pl.ds(pl.multiple_of(f * rows, rows), rows)
    loads = [
        pltpu.make_async_copy(a, b, in_s.at[i])
        for i, (a, b) in enumerate((
            (w_hbm, wfull.at[own_rows, :]), (ta_hbm, ta2.at[0:tokens, :]), (g_hbm, g_ref), (q_hbm, q_ref),
            (nk_hbm, nk_ref), (nv_hbm, nv_ref), (ck_hbm, ck_ref), (cv_hbm, cv_ref),
        ))
    ]
    barrier = pltpu.get_barrier_semaphore()
    for dev in (zp, zm, zp2, zm2, xp, gp):
        pl.semaphore_signal(barrier, inc=1, device_id=dev, device_id_type=MESH)

    def greet(k, _):
        pl.semaphore_signal(barrier, inc=1, device_id=(f, peer(k)), device_id_type=MESH)
        return 0

    lax.fori_loop(1, tp, greet, 0)
    for load in loads:
        load.start()

    def remote(src, dst, s_sem, r_sem, dev):
        return pltpu.make_async_remote_copy(
            src_ref=src, dst_ref=dst, send_sem=s_sem, recv_sem=r_sem,
            device_id=dev, device_id_type=MESH,
        )

    def shard(owner):
        return wfull.at[pl.ds(pl.multiple_of((xl * ring + owner) * rows, rows), rows), :]

    def even_owner(d, s):
        return (z + ring - 2 * s) % ring if d == 0 else (z + 2 * s) % ring

    def odd_owner(d, k):
        return (z + ring - 2 * k - 1) % ring if d == 0 else (z + 2 * k + 1) % ring

    def ag(d, s, first=False):
        place = shard(even_owner(d, s - 1))
        return remote(w_hbm if first else place, place, ag_s.at[d, s - 1], ag_r.at[d, s - 1],
                      zp2 if d == 0 else zm2)

    def fw(d, k, first=False):
        place = shard(even_owner(d, k))
        return remote(w_hbm if first else place, place, fw_s.at[d, k], fw_r.at[d, k],
                      zp if d == 0 else zm)

    def ax(owner, first=False):
        place = shard(owner)
        k = (owner + ring - z) % ring
        return remote(w_hbm if first else place, place, ax_s.at[k], ax_r.at[k], xp)

    def block(owner, h):
        return part.at[pl.ds(pl.multiple_of(owner * rows, rows), rows), h * hcols:(h + 1) * hcols]

    def ahead(d, distance):
        return (z + distance) % ring if d == 0 else (z + ring - distance) % ring

    def nb(d, k):
        return remote(nbs.at[d, k], nbr.at[d, k], nb_s.at[d, k], nb_r.at[d, k],
                      zp if d == 0 else zm)

    def send_nb(d, k):
        for h in range(2):
            nbs[d, k, :, h * hcols:(h + 1) * hcols] = (
                block(ahead(d, 2 * k + 1), h)[...].astype(NEAR)
            )
        nb(d, k).start()

    def bufs(s):
        return (snd16, rcv16) if s <= NARROW_HOPS else (snd32, rcv32)

    def rs(d, h, s):
        src, dst = bufs(s)
        return remote(src.at[d, h, s - 1], dst.at[d, h, s - 1], rs_s.at[d, h, s - 1],
                      rs_r.at[d, h, s - 1], zp2 if d == 0 else zm2)

    def rs_step(d, s):
        k = hops - s + 1 - d
        if k < hops:
            nb(d, k).wait_recv()
        for h in range(2):
            total = block(ahead(d, 2 * k), h)[...]
            if k < hops:
                total += nbr[d, k, :, h * hcols:(h + 1) * hcols].astype(F32)
            if s > 1:
                rs(d, h, s - 1).wait_recv()
                total += bufs(s - 1)[1][d, h, s - 2].astype(F32)
            src = bufs(s)[0]
            src[d, h, s - 1] = total.astype(src.dtype)
            rs(d, h, s).start()

    def pair_of(i):
        off = ((i + 1) // 2) * (1 - 2 * ((i + 1) % 2))
        return ((z + half) // 2 + off + ring) % half

    def gx(i):
        at = pl.multiple_of((1 - xl) * span + pair_of(i) * (2 * rows), 2 * rows)
        return remote(g_hbm.at[:, pl.ds(at, 2 * rows)], gin.at[i], g_s.at[i], g_r.at[i], gp)

    tax = remote(ta_hbm, ta2.at[tokens:2 * tokens, :], t_s, t_r, xp)

    def axa(k):
        return remote(sa.at[peer(k)], ra.at[t], a_s.at[k - 1], a_r.at[k - 1], (f, peer(k)))

    def axb(k):
        return remote(sb.at[peer(k)], rb.at[t], b_s.at[k - 1], b_r.at[k - 1], (f, peer(k)))

    def tdot(a, b):
        return lax.dot_general(a, b, (((0,), (0,)), ((), ())), preferred_element_type=F32)

    def ndot(a, b):
        return lax.dot_general(a, b, (((1,), (1,)), ((), ())), preferred_element_type=F32)

    pl.semaphore_wait(barrier, 6 + tp - 1)

    ag(0, 1, True).start()
    ag(1, 1, True).start()
    fw(0, 0, True).start()
    fw(1, 0, True).start()
    tax.start()
    gx(0).start()
    gx(1).start()
    gx(2).start()
    gx(3).start()
    ax(z, True).start()

    def send_g(i, _):
        gx(i).start()
        return 0

    lax.fori_loop(4, half, send_g, 0)

    for i in (3, 4, 5, 6, 7):
        loads[i].wait()

    qf = q_ref[0].astype(F32)
    for h in range(heads):
        qs[h * steps:(h + 1) * steps, :] = qf[:, h * HD:(h + 1) * HD]
    scaling = 1.0 / HD**0.5
    length = len_ref[0]
    span_q = group * steps
    npos = ck_ref.shape[1]
    pos = t * npos + lax.broadcasted_iota(jnp.int32, (span_q, npos), 1)
    ok = pos < length
    step_of = lax.broadcasted_iota(jnp.int32, (span_q, 1), 0) % steps
    for g in range(kv_heads):
        lanes = slice(g * HD, (g + 1) * HD)
        q32 = qs[g * span_q:(g + 1) * span_q, :]
        sc = ndot(q32.astype(BF16), ck_ref[0, :, lanes]) * scaling
        sc = jnp.where(ok, sc, NEG_FILL)
        new = []
        top = jnp.max(sc, axis=-1, keepdims=True)
        for j in range(steps):
            key = nk_ref[0, j:j + 1, lanes].astype(F32)
            sj = jnp.sum(q32 * key, axis=-1, keepdims=True) * scaling
            oj = jnp.logical_and(step_of >= j, t == 0)
            sj = jnp.where(oj, sj, NEG_FILL)
            new.append((sj, oj))
            top = jnp.maximum(top, sj)
        pr = jnp.where(ok, jnp.exp(sc - top), 0.0)
        hi = pr.astype(BF16)
        lo = (pr - hi.astype(F32)).astype(BF16)
        val = cv_ref[0, :, lanes]
        wt = jnp.dot(hi, val, preferred_element_type=F32) + jnp.dot(
            lo, val, preferred_element_type=F32
        )
        tot = jnp.sum(pr, axis=-1, keepdims=True)
        for j in range(steps):
            sj, oj = new[j]
            pj = jnp.where(oj, jnp.exp(sj - top), 0.0)
            tot = tot + pj
            wt = wt + pj * nv_ref[0, j:j + 1, lanes].astype(F32)
        topb = jnp.broadcast_to(top, (span_q, HD))
        totb = jnp.broadcast_to(tot, (span_q, HD))
        for j in range(group // heads_dev):
            dest = g * (group // heads_dev) + j
            mine = slice(j * unit, (j + 1) * unit)
            sa[dest, 0:unit, :] = wt[mine]
            sa[dest, unit:2 * unit, :] = topb[mine]
            sa[dest, 2 * unit:3 * unit, :] = totb[mine]
    ra[t] = sa[t]

    def send_a(k, _):
        axa(k).start()
        return 0

    lax.fori_loop(1, tp, send_a, 0)

    def ag_step(s, mode):
        for d in range(2 if mode > 0 else 1):
            ag(d, s).wait_recv()
            if mode == 2 or (mode == 1 and d == 0):
                ag(d, s + 1).start()
            if mode > 0:
                fw(d, s).start()
            ax(even_owner(d, s)).start()
        for d in range(2):
            fw(d, s - 1).wait_recv()
            ax(odd_owner(d, s - 1)).start()

    def g_step(i):
        gx(i).wait_recv()
        pair = pair_of(i)
        at = pl.multiple_of(xl * span + pair * (2 * rows), 2 * rows)
        both = jnp.concatenate([g_ref[:, pl.ds(at, 2 * rows)], gin[i]], axis=0)
        here = pl.ds(pl.multiple_of(pair * (2 * rows), 2 * rows), 2 * rows)
        part[here, :] = tdot(both, ta2[...])

    per_dest = dcols // (2 * rows)

    def use_pair(n):
        off = ((n + 1) // 2) * (1 - 2 * ((n + 1) % 2))
        pair = (z // 2 + off + half) % half
        for e in range(2):
            ax((2 * pair + e) % ring).wait_recv()
        places, gs, ws = [], [], []
        for c in (xl, 1 - xl):
            place = c * half + pair
            at = pl.ds(pl.multiple_of(place * (2 * rows), 2 * rows), 2 * rows)
            places.append(place)
            gs.append(g_ref[:, at])
            ws.append(wfull[at, :])
        wide = jnp.concatenate(ws, axis=0)
        gacc[...] += jnp.dot(
            jnp.concatenate(gs, axis=1), wide, preferred_element_type=F32
        )
        out = ndot(att[...].astype(BF16), wide)[0:8]
        for e, place in enumerate(places):
            lane = pl.ds(pl.multiple_of((place % per_dest) * (2 * rows), 2 * rows), 2 * rows)
            sb[place // per_dest, :, lane] = out[:, e * 2 * rows:(e + 1) * 2 * rows]

    for i in (0, 1, 2):
        loads[i].wait()
    ag_step(1, min(hops - 1, 2))
    tax.wait_recv()
    for i in range(4):
        g_step(i)
    for d in range(2):
        send_nb(d, hops - 1)
    gacc[...] = jnp.zeros_like(gacc)

    def combine():
        def wait_a(k, _):
            axa(k).wait_recv()
            return 0

        lax.fori_loop(1, tp, wait_a, 0)
        tops = ra[:, unit:2 * unit, :]
        scale = jnp.exp(tops - jnp.max(tops, axis=0, keepdims=True))
        total = jnp.sum(ra[:, 2 * unit:3 * unit, :] * scale, axis=0)
        mixed = jnp.sum(ra[:, 0:unit, :] * scale, axis=0) / total
        att[...] = jnp.zeros_like(att)
        for hh in range(heads_dev):
            att[0:steps, hh * HD:(hh + 1) * HD] = mixed[hh * steps:(hh + 1) * steps]

    def send_b(k, _):
        axb(k).start()
        return 0

    used = 0
    for s in range(1, hops + 1):
        rs_step(0, s)
        if s < hops:
            rs_step(1, s)
        if s < hops:
            ag_step(s + 1, min(hops - s - 1, 2))
        for i in (2 * s + 2, 2 * s + 3):
            if i < half:
                g_step(i)
        if s < hops:
            for d in range(2):
                send_nb(d, hops - 1 - s)
        if s == 3:
            combine()
        if s > 3:
            more = min(3, 2 * s - 2 - used)
            lax.fori_loop(used, used + more, lambda n, c: (use_pair(n), c)[1], 0)
            used += more
    if hops <= 3:
        combine()
    lax.fori_loop(used, half, lambda n, c: (use_pair(n), c)[1], 0)
    lax.fori_loop(1, tp, send_b, 0)
    rb[t] = sb[t]
    ga_ref[...] = gacc[...].astype(BF16)

    for d in range(2):
        nb(d, 0).wait_recv()
    for h in range(2):
        at = slice(h * hcols, (h + 1) * hcols)
        total = block(z, h)[...] + nbr[0, 0, :, at].astype(F32) + nbr[1, 0, :, at].astype(F32)
        for d in range(2):
            rs(d, h, hops - d).wait_recv()
            total += bufs(hops - d)[1][d, h, hops - d - 1].astype(F32)
        gw_ref[:, at] = total

    def wait_b(k, _):
        axb(k).wait_recv()
        return 0

    lax.fori_loop(1, tp, wait_b, 0)
    dec_ref[0] = jnp.sum(rb[...], axis=0)[0:steps].astype(BF16)

    tax.wait_send()

    def drain_tp(k, _):
        axa(k).wait_send()
        axb(k).wait_send()
        return 0

    lax.fori_loop(1, tp, drain_tp, 0)

    def drain_g(i, _):
        gx(i).wait_send()
        return 0

    lax.fori_loop(0, half, drain_g, 0)

    def drain_x(k, _):
        ax((z + k) % ring).wait_send()
        return 0

    lax.fori_loop(0, ring, drain_x, 0)
    for d in range(2):
        def drain_z(s, _, d=d):
            ag(d, s).wait_send()
            return 0

        lax.fori_loop(1, hops + 1 - d, drain_z, 0)

        def drain_f(k, _, d=d):
            fw(d, k).wait_send()
            return 0

        lax.fori_loop(0, hops, drain_f, 0)
        def drain_n(k, _, d=d):
            nb(d, k).wait_send()
            return 0

        lax.fori_loop(0, hops, drain_n, 0)
        for h in range(2):
            for s in range(1, hops + 1 - d):
                rs(d, h, s).wait_send()


def solution(mesh):
    fs, tp = mesh.shape["fsdp"], mesh.shape["tp"]
    ring = fs // 2
    half = ring // 2
    hops = half // 2

    def shards(q, nk, nv, ck, cv, lengths, w, ta, g):
        rows, cols = w.shape
        tokens = ta.shape[0]
        heads = q.shape[2] // HD
        steps = q.shape[1]
        dcols = fs * rows // tp
        dma = pltpu.SemaphoreType.DMA
        vmem = pl.BlockSpec(memory_space=pltpu.VMEM)
        hbm = pl.BlockSpec(memory_space=pltpu.HBM)
        smem = pl.BlockSpec(memory_space=pltpu.SMEM)
        return pl.pallas_call(
            functools.partial(kernel, fs, tp),
            out_shape=(
                jax.ShapeDtypeStruct((1, steps, dcols), BF16),
                jax.ShapeDtypeStruct((tokens, cols), BF16),
                jax.ShapeDtypeStruct((rows, cols), F32),
            ),
            in_specs=[hbm] * 5 + [smem] + [hbm] * 3,
            out_specs=(vmem,) * 3,
            scratch_shapes=[
                pltpu.VMEM(q.shape, BF16), pltpu.VMEM(nk.shape, BF16), pltpu.VMEM(nv.shape, BF16),
                pltpu.VMEM(ck.shape, BF16), pltpu.VMEM(cv.shape, BF16),
                pltpu.VMEM((2 * tokens, cols), BF16), pltpu.VMEM(g.shape, BF16), dma((8,)),
                pltpu.VMEM((fs * rows, cols), BF16),
                pltpu.VMEM((ring * rows, cols), F32),
                pltpu.VMEM((tokens, cols), F32),
                pltpu.VMEM((half, tokens, 2 * rows), BF16),
                pltpu.VMEM((2, hops, rows, cols), NEAR), pltpu.VMEM((2, hops, rows, cols), NEAR),
                pltpu.VMEM((2, 2, hops, rows, cols // 2), BF16),
                pltpu.VMEM((2, 2, hops, rows, cols // 2), BF16),
                pltpu.VMEM((2, 2, hops, rows, cols // 2), F32),
                pltpu.VMEM((2, 2, hops, rows, cols // 2), F32),
                pltpu.VMEM((heads * steps, HD), F32),
                pltpu.VMEM((16, cols), F32),
                pltpu.VMEM((tp, 16, HD), F32),
                pltpu.VMEM((tp, 16, HD), F32),
                pltpu.VMEM((tp, 8, dcols), F32),
                pltpu.VMEM((tp, 8, dcols), F32),
                dma((2, hops)), dma((2, hops)),
                dma((2, hops)), dma((2, hops)),
                dma((ring,)), dma((ring,)),
                dma((2, hops)), dma((2, hops)),
                dma((2, 2, hops)), dma((2, 2, hops)),
                dma((half,)), dma((half,)),
                dma, dma,
                dma((tp - 1,)), dma((tp - 1,)),
                dma((tp - 1,)), dma((tp - 1,)),
            ],
            compiler_params=pltpu.CompilerParams(
                collective_id=0, has_side_effects=True, vmem_limit_bytes=48 * 1024 * 1024
            ),
        )(*[pltpu.with_memory_space_constraint(a, pltpu.HBM) for a in (q, nk, nv, ck, cv)],
          lengths, *[pltpu.with_memory_space_constraint(a, pltpu.HBM) for a in (w, ta, g)])

    return jax.shard_map(
        shards,
        mesh=mesh,
        in_specs=(
            P("fsdp", None, None), P("fsdp", None, None), P("fsdp", None, None),
            P("fsdp", "tp", None), P("fsdp", "tp", None), P("fsdp"),
            P("fsdp", "tp"), P("fsdp", "tp"), P("fsdp", None),
        ),
        out_specs=(P("fsdp", None, "tp"), P("fsdp", "tp"), P("fsdp", "tp")),
        check_vma=False,
    )
```

```python
import functools

import jax
import jax.numpy as jnp
from jax import lax
from jax.experimental import pallas as pl
from jax.experimental.pallas import tpu as pltpu
from jax.sharding import PartitionSpec as P

HD = 128
NEG_FILL = -1e30
MESH = pl.DeviceIdType.MESH
F32 = jnp.float32
BF16 = jnp.bfloat16
NEAR = BF16
NARROW_HOPS = 4


def kernel(
    fs, tp,
    q_hbm, nk_hbm, nv_hbm, ck_hbm, cv_hbm, len_ref, w_hbm, ta_hbm, g_hbm,
    dec_ref, ga_ref, gw_ref,
    q_ref, nk_ref, nv_ref, ck_ref, cv_ref, ta2, g_ref, in_s,
    wfull, part, gacc, gin, nbs, nbr, snd16, rcv16, snd32, rcv32, qs, att, sa, ra, sb, rb,
    ag_s, ag_r, fw_s, fw_r, ax_s, ax_r, nb_s, nb_r, rs_s, rs_r, g_s, g_r, t_s, t_r, a_s, a_r, b_s, b_r,
):
    ring = fs // 2
    half = ring // 2
    hops = half // 2
    rows = w_hbm.shape[0]
    cols = w_hbm.shape[1]
    tokens = ta_hbm.shape[0]
    hcols = cols // 2
    steps = q_ref.shape[1]
    heads = q_ref.shape[2] // HD
    kv_heads = nk_ref.shape[2] // HD
    group = heads // kv_heads
    heads_dev = heads // tp
    unit = heads_dev * steps
    dout = fs * rows
    dcols = dout // tp
    span = ring * rows

    f = lax.axis_index("fsdp")
    t = lax.axis_index("tp")
    xl = f // ring
    z = f % ring
    zp = (xl * ring + (z + 1) % ring, t)
    zm = (xl * ring + (z + ring - 1) % ring, t)
    zp2 = (xl * ring + (z + 2) % ring, t)
    zm2 = (xl * ring + (z + ring - 2) % ring, t)
    xp = ((f + ring) % fs, t)
    gp = ((f + ring) % fs, (t + tp // 2) % tp)

    def peer(k):
        return (t + k) % tp

    own_rows = pl.ds(pl.multiple_of(f * rows, rows), rows)
    loads = [
        pltpu.make_async_copy(a, b, in_s.at[i])
        for i, (a, b) in enumerate((
            (w_hbm, wfull.at[own_rows, :]), (ta_hbm, ta2.at[0:tokens, :]), (g_hbm, g_ref), (q_hbm, q_ref),
            (nk_hbm, nk_ref), (nv_hbm, nv_ref), (ck_hbm, ck_ref), (cv_hbm, cv_ref),
        ))
    ]
    barrier = pltpu.get_barrier_semaphore()
    for dev in (zp, zm, zp2, zm2, xp, gp):
        pl.semaphore_signal(barrier, inc=1, device_id=dev, device_id_type=MESH)

    def greet(k, _):
        pl.semaphore_signal(barrier, inc=1, device_id=(f, peer(k)), device_id_type=MESH)
        return 0

    lax.fori_loop(1, tp, greet, 0)
    for load in loads:
        load.start()

    def remote(src, dst, s_sem, r_sem, dev):
        return pltpu.make_async_remote_copy(
            src_ref=src, dst_ref=dst, send_sem=s_sem, recv_sem=r_sem,
            device_id=dev, device_id_type=MESH,
        )

    def shard(owner):
        return wfull.at[pl.ds(pl.multiple_of((xl * ring + owner) * rows, rows), rows), :]

    def even_owner(d, s):
        return (z + ring - 2 * s) % ring if d == 0 else (z + 2 * s) % ring

    def odd_owner(d, k):
        return (z + ring - 2 * k - 1) % ring if d == 0 else (z + 2 * k + 1) % ring

    def ag(d, s, first=False):
        place = shard(even_owner(d, s - 1))
        return remote(w_hbm if first else place, place, ag_s.at[d, s - 1], ag_r.at[d, s - 1],
                      zp2 if d == 0 else zm2)

    def fw(d, k, first=False):
        place = shard(even_owner(d, k))
        return remote(w_hbm if first else place, place, fw_s.at[d, k], fw_r.at[d, k],
                      zp if d == 0 else zm)

    def ax(owner, first=False):
        place = shard(owner)
        k = (owner + ring - z) % ring
        return remote(w_hbm if first else place, place, ax_s.at[k], ax_r.at[k], xp)

    def block(owner, h):
        return part.at[pl.ds(pl.multiple_of(owner * rows, rows), rows), h * hcols:(h + 1) * hcols]

    def ahead(d, distance):
        return (z + distance) % ring if d == 0 else (z + ring - distance) % ring

    def nb(d, k):
        return remote(nbs.at[d, k], nbr.at[d, k], nb_s.at[d, k], nb_r.at[d, k],
                      zp if d == 0 else zm)

    def send_nb(d, k):
        for h in range(2):
            nbs[d, k, :, h * hcols:(h + 1) * hcols] = (
                block(ahead(d, 2 * k + 1), h)[...].astype(NEAR)
            )
        nb(d, k).start()

    def bufs(s):
        return (snd16, rcv16) if s <= NARROW_HOPS else (snd32, rcv32)

    def rs(d, h, s):
        src, dst = bufs(s)
        return remote(src.at[d, h, s - 1], dst.at[d, h, s - 1], rs_s.at[d, h, s - 1],
                      rs_r.at[d, h, s - 1], zp2 if d == 0 else zm2)

    def rs_step(d, s):
        k = hops - s + 1 - d
        if k < hops:
            nb(d, k).wait_recv()
        for h in range(2):
            total = block(ahead(d, 2 * k), h)[...]
            if k < hops:
                total += nbr[d, k, :, h * hcols:(h + 1) * hcols].astype(F32)
            if s > 1:
                rs(d, h, s - 1).wait_recv()
                total += bufs(s - 1)[1][d, h, s - 2].astype(F32)
            src = bufs(s)[0]
            src[d, h, s - 1] = total.astype(src.dtype)
            rs(d, h, s).start()

    def pair_of(i):
        off = ((i + 1) // 2) * (1 - 2 * ((i + 1) % 2))
        return ((z + half) // 2 + off + ring) % half

    def gx(i):
        at = pl.multiple_of((1 - xl) * span + pair_of(i) * (2 * rows), 2 * rows)
        return remote(g_hbm.at[:, pl.ds(at, 2 * rows)], gin.at[i], g_s.at[i], g_r.at[i], gp)

    tax = remote(ta_hbm, ta2.at[tokens:2 * tokens, :], t_s, t_r, xp)

    def axa(k):
        return remote(sa.at[peer(k)], ra.at[t], a_s.at[k - 1], a_r.at[k - 1], (f, peer(k)))

    def axb(k):
        return remote(sb.at[peer(k)], rb.at[t], b_s.at[k - 1], b_r.at[k - 1], (f, peer(k)))

    def tdot(a, b):
        return lax.dot_general(a, b, (((0,), (0,)), ((), ())), preferred_element_type=F32)

    def ndot(a, b):
        return lax.dot_general(a, b, (((1,), (1,)), ((), ())), preferred_element_type=F32)

    pl.semaphore_wait(barrier, 6 + tp - 1)

    ag(0, 1, True).start()
    ag(1, 1, True).start()
    fw(0, 0, True).start()
    fw(1, 0, True).start()
    tax.start()
    gx(0).start()
    gx(1).start()
    gx(2).start()
    gx(3).start()
    ax(z, True).start()

    def send_g(i, _):
        gx(i).start()
        return 0

    lax.fori_loop(4, half, send_g, 0)

    for i in (3, 4, 5, 6, 7):
        loads[i].wait()

    qf = q_ref[0].astype(F32)
    for h in range(heads):
        qs[h * steps:(h + 1) * steps, :] = qf[:, h * HD:(h + 1) * HD]
    scaling = 1.0 / HD**0.5
    length = len_ref[0]
    span_q = group * steps
    npos = ck_ref.shape[1]
    pos = t * npos + lax.broadcasted_iota(jnp.int32, (span_q, npos), 1)
    ok = pos < length
    step_of = lax.broadcasted_iota(jnp.int32, (span_q, 1), 0) % steps
    for g in range(kv_heads):
        lanes = slice(g * HD, (g + 1) * HD)
        q32 = qs[g * span_q:(g + 1) * span_q, :]
        sc = ndot(q32.astype(BF16), ck_ref[0, :, lanes]) * scaling
        sc = jnp.where(ok, sc, NEG_FILL)
        new = []
        top = jnp.max(sc, axis=-1, keepdims=True)
        for j in range(steps):
            key = nk_ref[0, j:j + 1, lanes].astype(F32)
            sj = jnp.sum(q32 * key, axis=-1, keepdims=True) * scaling
            oj = jnp.logical_and(step_of >= j, t == 0)
            sj = jnp.where(oj, sj, NEG_FILL)
            new.append((sj, oj))
            top = jnp.maximum(top, sj)
        pr = jnp.where(ok, jnp.exp(sc - top), 0.0)
        hi = pr.astype(BF16)
        lo = (pr - hi.astype(F32)).astype(BF16)
        val = cv_ref[0, :, lanes]
        wt = jnp.dot(hi, val, preferred_element_type=F32) + jnp.dot(
            lo, val, preferred_element_type=F32
        )
        tot = jnp.sum(pr, axis=-1, keepdims=True)
        for j in range(steps):
            sj, oj = new[j]
            pj = jnp.where(oj, jnp.exp(sj - top), 0.0)
            tot = tot + pj
            wt = wt + pj * nv_ref[0, j:j + 1, lanes].astype(F32)
        topb = jnp.broadcast_to(top, (span_q, HD))
        totb = jnp.broadcast_to(tot, (span_q, HD))
        for j in range(group // heads_dev):
            dest = g * (group // heads_dev) + j
            mine = slice(j * unit, (j + 1) * unit)
            sa[dest, 0:unit, :] = wt[mine]
            sa[dest, unit:2 * unit, :] = topb[mine]
            sa[dest, 2 * unit:3 * unit, :] = totb[mine]
    ra[t] = sa[t]

    def send_a(k, _):
        axa(k).start()
        return 0

    lax.fori_loop(1, tp, send_a, 0)

    def ag_step(s, mode):
        for d in range(2 if mode > 0 else 1):
            ag(d, s).wait_recv()
            if mode == 2 or (mode == 1 and d == 0):
                ag(d, s + 1).start()
            if mode > 0:
                fw(d, s).start()
            ax(even_owner(d, s)).start()
        for d in range(2):
            fw(d, s - 1).wait_recv()
            ax(odd_owner(d, s - 1)).start()

    def g_step(i):
        gx(i).wait_recv()
        pair = pair_of(i)
        at = pl.multiple_of(xl * span + pair * (2 * rows), 2 * rows)
        both = jnp.concatenate([g_ref[:, pl.ds(at, 2 * rows)], gin[i]], axis=0)
        here = pl.ds(pl.multiple_of(pair * (2 * rows), 2 * rows), 2 * rows)
        part[here, :] = tdot(both, ta2[...])

    per_dest = dcols // (2 * rows)

    def use_pair(n):
        off = ((n + 1) // 2) * (1 - 2 * ((n + 1) % 2))
        pair = (z // 2 + off + half) % half
        for e in range(2):
            ax((2 * pair + e) % ring).wait_recv()
        places, gs, ws = [], [], []
        for c in (xl, 1 - xl):
            place = c * half + pair
            at = pl.ds(pl.multiple_of(place * (2 * rows), 2 * rows), 2 * rows)
            places.append(place)
            gs.append(g_ref[:, at])
            ws.append(wfull[at, :])
        wide = jnp.concatenate(ws, axis=0)
        gacc[...] += jnp.dot(
            jnp.concatenate(gs, axis=1), wide, preferred_element_type=F32
        )
        out = ndot(att[...].astype(BF16), wide)[0:8]
        for e, place in enumerate(places):
            lane = pl.ds(pl.multiple_of((place % per_dest) * (2 * rows), 2 * rows), 2 * rows)
            sb[place // per_dest, :, lane] = out[:, e * 2 * rows:(e + 1) * 2 * rows]

    for i in (0, 1, 2):
        loads[i].wait()
    ag_step(1, min(hops - 1, 2))
    tax.wait_recv()
    for i in range(4):
        g_step(i)
    for d in range(2):
        send_nb(d, hops - 1)
    gacc[...] = jnp.zeros_like(gacc)

    def combine():
        def wait_a(k, _):
            axa(k).wait_recv()
            return 0

        lax.fori_loop(1, tp, wait_a, 0)
        tops = ra[:, unit:2 * unit, :]
        scale = jnp.exp(tops - jnp.max(tops, axis=0, keepdims=True))
        total = jnp.sum(ra[:, 2 * unit:3 * unit, :] * scale, axis=0)
        mixed = jnp.sum(ra[:, 0:unit, :] * scale, axis=0) / total
        att[...] = jnp.zeros_like(att)
        for hh in range(heads_dev):
            att[0:steps, hh * HD:(hh + 1) * HD] = mixed[hh * steps:(hh + 1) * steps]

    def send_b(k, _):
        axb(k).start()
        return 0

    used = 0
    for s in range(1, hops + 1):
        if s == 1:
            rs_step(0, s)
            rs_step(1, s)
        if s < hops:
            ag_step(s + 1, min(hops - s - 1, 2))
        if s > 1:
            rs_step(0, s)
            if s < hops:
                rs_step(1, s)
        for i in (2 * s + 2, 2 * s + 3):
            if i < half:
                g_step(i)
        if s < hops:
            for d in range(2):
                send_nb(d, hops - 1 - s)
        if s == 3:
            combine()
        if s > 3:
            more = min(3, 2 * s - 2 - used)
            lax.fori_loop(used, used + more, lambda n, c: (use_pair(n), c)[1], 0)
            used += more
    if hops <= 3:
        combine()
    lax.fori_loop(used, half, lambda n, c: (use_pair(n), c)[1], 0)
    lax.fori_loop(1, tp, send_b, 0)
    rb[t] = sb[t]
    ga_ref[...] = gacc[...].astype(BF16)

    for d in range(2):
        nb(d, 0).wait_recv()
    for h in range(2):
        at = slice(h * hcols, (h + 1) * hcols)
        total = block(z, h)[...] + nbr[0, 0, :, at].astype(F32) + nbr[1, 0, :, at].astype(F32)
        for d in range(2):
            rs(d, h, hops - d).wait_recv()
            total += bufs(hops - d)[1][d, h, hops - d - 1].astype(F32)
        gw_ref[:, at] = total

    def wait_b(k, _):
        axb(k).wait_recv()
        return 0

    lax.fori_loop(1, tp, wait_b, 0)
    dec_ref[0] = jnp.sum(rb[...], axis=0)[0:steps].astype(BF16)

    tax.wait_send()

    def drain_tp(k, _):
        axa(k).wait_send()
        axb(k).wait_send()
        return 0

    lax.fori_loop(1, tp, drain_tp, 0)

    def drain_g(i, _):
        gx(i).wait_send()
        return 0

    lax.fori_loop(0, half, drain_g, 0)

    def drain_x(k, _):
        ax((z + k) % ring).wait_send()
        return 0

    lax.fori_loop(0, ring, drain_x, 0)
    for d in range(2):
        def drain_z(s, _, d=d):
            ag(d, s).wait_send()
            return 0

        lax.fori_loop(1, hops + 1 - d, drain_z, 0)

        def drain_f(k, _, d=d):
            fw(d, k).wait_send()
            return 0

        lax.fori_loop(0, hops, drain_f, 0)
        def drain_n(k, _, d=d):
            nb(d, k).wait_send()
            return 0

        lax.fori_loop(0, hops, drain_n, 0)
        for h in range(2):
            for s in range(1, hops + 1 - d):
                rs(d, h, s).wait_send()


def solution(mesh):
    fs, tp = mesh.shape["fsdp"], mesh.shape["tp"]
    ring = fs // 2
    half = ring // 2
    hops = half // 2

    def shards(q, nk, nv, ck, cv, lengths, w, ta, g):
        rows, cols = w.shape
        tokens = ta.shape[0]
        heads = q.shape[2] // HD
        steps = q.shape[1]
        dcols = fs * rows // tp
        dma = pltpu.SemaphoreType.DMA
        vmem = pl.BlockSpec(memory_space=pltpu.VMEM)
        hbm = pl.BlockSpec(memory_space=pltpu.HBM)
        smem = pl.BlockSpec(memory_space=pltpu.SMEM)
        return pl.pallas_call(
            functools.partial(kernel, fs, tp),
            out_shape=(
                jax.ShapeDtypeStruct((1, steps, dcols), BF16),
                jax.ShapeDtypeStruct((tokens, cols), BF16),
                jax.ShapeDtypeStruct((rows, cols), F32),
            ),
            in_specs=[hbm] * 5 + [smem] + [hbm] * 3,
            out_specs=(vmem,) * 3,
            scratch_shapes=[
                pltpu.VMEM(q.shape, BF16), pltpu.VMEM(nk.shape, BF16), pltpu.VMEM(nv.shape, BF16),
                pltpu.VMEM(ck.shape, BF16), pltpu.VMEM(cv.shape, BF16),
                pltpu.VMEM((2 * tokens, cols), BF16), pltpu.VMEM(g.shape, BF16), dma((8,)),
                pltpu.VMEM((fs * rows, cols), BF16),
                pltpu.VMEM((ring * rows, cols), F32),
                pltpu.VMEM((tokens, cols), F32),
                pltpu.VMEM((half, tokens, 2 * rows), BF16),
                pltpu.VMEM((2, hops, rows, cols), NEAR), pltpu.VMEM((2, hops, rows, cols), NEAR),
                pltpu.VMEM((2, 2, hops, rows, cols // 2), BF16),
                pltpu.VMEM((2, 2, hops, rows, cols // 2), BF16),
                pltpu.VMEM((2, 2, hops, rows, cols // 2), F32),
                pltpu.VMEM((2, 2, hops, rows, cols // 2), F32),
                pltpu.VMEM((heads * steps, HD), F32),
                pltpu.VMEM((16, cols), F32),
                pltpu.VMEM((tp, 16, HD), F32),
                pltpu.VMEM((tp, 16, HD), F32),
                pltpu.VMEM((tp, 8, dcols), F32),
                pltpu.VMEM((tp, 8, dcols), F32),
                dma((2, hops)), dma((2, hops)),
                dma((2, hops)), dma((2, hops)),
                dma((ring,)), dma((ring,)),
                dma((2, hops)), dma((2, hops)),
                dma((2, 2, hops)), dma((2, 2, hops)),
                dma((half,)), dma((half,)),
                dma, dma,
                dma((tp - 1,)), dma((tp - 1,)),
                dma((tp - 1,)), dma((tp - 1,)),
            ],
            compiler_params=pltpu.CompilerParams(
                collective_id=0, has_side_effects=True, vmem_limit_bytes=48 * 1024 * 1024
            ),
        )(*[pltpu.with_memory_space_constraint(a, pltpu.HBM) for a in (q, nk, nv, ck, cv)],
          lengths, *[pltpu.with_memory_space_constraint(a, pltpu.HBM) for a in (w, ta, g)])

    return jax.shard_map(
        shards,
        mesh=mesh,
        in_specs=(
            P("fsdp", None, None), P("fsdp", None, None), P("fsdp", None, None),
            P("fsdp", "tp", None), P("fsdp", "tp", None), P("fsdp"),
            P("fsdp", "tp"), P("fsdp", "tp"), P("fsdp", None),
        ),
        out_specs=(P("fsdp", None, "tp"), P("fsdp", "tp"), P("fsdp", "tp")),
        check_vma=False,
    )
```
